1024 devices in a mesh: energy: 16 (over z, core), slab: 64 (over x, y).
Axes of the slice: x: 8, y: 8, z: 8, core: 2. Of those that a mesh axis runs over, the one named last changes fastest.
Arguments:
- green_less: bfloat16 [32, 64, 2, 256, 256], P('energy', 'slab'), may hold values from -6 to 6
- green_ret: bfloat16 [32, 64, 2, 256, 256], P('energy', 'slab'), may hold values from -0.375 to 0.375
- hamilton: bfloat16 [64, 256, 256], P('slab'), may hold values from -0.375 to 0.375
- coupling: bfloat16 [4, 256, 256], replicated, may hold values from -3 to 3
- occupation: float32 [4], replicated, may hold values from 0.2 to 2
- shifts: int32 [4], replicated, may hold values from 1 to 2, as said below
- interface: bfloat16 [2, 64, 64], replicated, may hold values from -0.75 to 0.75
Outputs:
- lesser_new: bfloat16 [32, 64, 2, 256, 256], P('energy', 'slab')
- chain: float32 [32, 64, 2, 64, 64], P('energy', 'slab')
The draws below stay inside these ranges and needn't reach their ends.
Inputs may be any that keep to these rules, and one draw needn't show every extreme that they name: `shifts`: every mode's shift is a positive whole number of grid points, and some mode has shift 2.
All inputs are finite; a program needn't handle non-finite values.
Results may differ from the reference program's by a relative error of at most 0.0017.
The reference program's roundings to bfloat16 on the way count: a program that leaves them out, or rounds other values in their place, can miss the bound.
Values may be sent and summed in bfloat16 or wider, within the bound.
A program may use at most 32 MiB of HBM per device.

```python
import math
import jax
import jax.numpy as jnp
from jax import lax

ORB = 256
NB = 64
MODES = 4
KSPAN = 2
NE = 32
SLABS = 64


def draw_shifts(key, part):
    first, second = jax.random.split(jax.random.fold_in(key, 17))
    base = jax.random.randint(first, (MODES,), 1, KSPAN + 1)
    picked = jax.random.randint(second, (), 0, MODES)
    return jnp.where(jnp.arange(MODES) == picked, KSPAN, base).astype(jnp.int32)


def steps_of(key, extent, cuts, least, top_value):
    level = 1.0
    for axis_at, blocks in cuts:
        steps = jax.random.uniform(jax.random.fold_in(jax.random.fold_in(key, 6), axis_at), (blocks,), jnp.float32, least / len(cuts), top_value / len(cuts))
        level = level * jnp.repeat(jnp.exp(steps), extent[axis_at] // blocks).reshape((-1,) + (1,) * (len(extent) - 1 - axis_at))
    return level


def bell_draw(rng, dims, deviation, reach, cuts=(), held_as=jnp.bfloat16):
    factor_of = steps_of(rng, dims, cuts, -0.22, 0.18) if cuts else 1.0
    values = jax.random.normal(rng, dims, jnp.float32) * deviation * factor_of
    return jnp.minimum(jnp.maximum(values, -reach), reach).astype(held_as)


def setup_inputs(seed: int = 0) -> dict:
    seeds = jax.random.split(jax.random.key(seed), 8)
    return {
        "green_less": bell_draw(seeds[0], (NE, SLABS, 2, ORB, ORB), 1.0, 6.0, ((0, 16), (1, 64))),
        "green_ret": bell_draw(seeds[1], (NE, SLABS, 2, ORB, ORB), ORB ** -0.5, 0.375, ((0, 16), (1, 64))),
        "hamilton": bell_draw(seeds[2], (SLABS, ORB, ORB), ORB ** -0.5, 0.375, ((0, 64),)),
        "coupling": bell_draw(seeds[3], (MODES, ORB, ORB), 0.2, 3.0),
        "occupation": jnp.clip(jnp.exp(jax.random.uniform(seeds[4], (MODES,), jnp.float32, math.log(0.2), math.log(2.0))), 0.2, 2.0),
        "shifts": draw_shifts(jax.random.fold_in(seeds[7], 71), 0),
        "interface": bell_draw(seeds[6], (2, NB, NB), NB ** -0.5, 0.75),
    }


eta = 2.0
high = lax.Precision.HIGHEST

def batch_mm(left, right):
    return jnp.einsum('eij,ejk->eik', left, right, precision=high)

def to_half(value):
    return lax.optimization_barrier(value.astype(jnp.bfloat16)).astype(jnp.float32)

def one_slab(less, ret, ham, coupling, occupation, shifts, interface, energies, scale):
    padded = jnp.pad(less.astype(jnp.float32), ((KSPAN, KSPAN), (0, 0), (0, 0), (0, 0)))
    total = jnp.zeros((NE, 2, ORB, ORB), jnp.float32)
    for mode in range(MODES):
        upper = lax.dynamic_slice_in_dim(padded, (KSPAN + shifts[mode]).astype(jnp.int32), NE, 0)
        lower = lax.dynamic_slice_in_dim(padded, (KSPAN - shifts[mode]).astype(jnp.int32), NE, 0)
        total = total + coupling[mode].astype(jnp.float32) * ((occupation[mode] + 1.0) * upper + occupation[mode] * lower)
    sigma = total.astype(jnp.bfloat16)
    ret_real = ret[:, 0].astype(jnp.float32)
    ret_imag = ret[:, 1].astype(jnp.float32)
    sig_real = sigma[:, 0].astype(jnp.float32)
    sig_imag = sigma[:, 1].astype(jnp.float32)
    half_real = batch_mm(ret_real, sig_real) - batch_mm(ret_imag, sig_imag)
    half_imag = batch_mm(ret_real, sig_imag) + batch_mm(ret_imag, sig_real)
    half_real = to_half(half_real)
    half_imag = to_half(half_imag)
    new_real = jnp.einsum('eij,ekj->eik', half_real, ret_real, precision=high) + jnp.einsum('eij,ekj->eik', half_imag, ret_imag, precision=high)
    new_imag = jnp.einsum('eij,ekj->eik', half_imag, ret_real, precision=high) - jnp.einsum('eij,ekj->eik', half_real, ret_imag, precision=high)
    lesser = jnp.stack([new_real, new_imag], 1).astype(jnp.bfloat16)
    ham_f = ham.astype(jnp.float32)
    mat_real = ham_f[None] + sig_real
    mat_imag = sig_imag
    diag_h = jnp.diagonal(ham_f)[NB:]
    offset = energies[:, None] - diag_h[None, :]
    denom = offset * offset + eta * eta
    inv_real = (offset / denom)[:, None, :]
    inv_imag = (-eta / denom)[:, None, :]
    left_real = mat_real[:, :NB, NB:]
    left_imag = mat_imag[:, :NB, NB:]
    q_real = to_half(left_real * inv_real - left_imag * inv_imag)
    q_imag = to_half(left_real * inv_imag + left_imag * inv_real)
    right_real = to_half(mat_real[:, NB:, :NB])
    right_imag = to_half(mat_imag[:, NB:, :NB])
    bound_real = to_half(mat_real[:, :NB, :NB] - (batch_mm(q_real, right_real) - batch_mm(q_imag, right_imag)))
    bound_imag = to_half(mat_imag[:, :NB, :NB] - (batch_mm(q_real, right_imag) + batch_mm(q_imag, right_real)))
    face = interface.astype(jnp.float32)
    face_real = jnp.broadcast_to(face[0], (NE, NB, NB))
    face_imag = jnp.broadcast_to(face[1], (NE, NB, NB))
    eye = jnp.eye(NB, dtype=jnp.float32)[None]
    fac_real = eye + scale * (batch_mm(bound_real, face_real) - batch_mm(bound_imag, face_imag))
    fac_imag = scale * (batch_mm(bound_real, face_imag) + batch_mm(bound_imag, face_real))
    return (lesser, jnp.stack([fac_real, fac_imag], 1))

def reference(green_less, green_ret, hamilton, coupling, occupation, shifts, interface):
    energies = -3.0 + 6.0 * (jnp.arange(NE).astype(jnp.float32) + 0.5) / NE
    scale = 1.0 / (8.0 * jnp.sqrt(jnp.float32(NB * SLABS)))

    def per_slab(index):
        less = lax.dynamic_index_in_dim(green_less, index, 1, keepdims=False)
        ret = lax.dynamic_index_in_dim(green_ret, index, 1, keepdims=False)
        ham = lax.dynamic_index_in_dim(hamilton, index, 0, keepdims=False)
        return one_slab(less, ret, ham, coupling, occupation, shifts, interface, energies, scale)
    lessers, factors = lax.map(per_slab, jnp.arange(SLABS).astype(jnp.int32))

    def step(carry, factor):
        prod_real = batch_mm(carry[0], factor[:, 0]) - batch_mm(carry[1], factor[:, 1])
        prod_imag = batch_mm(carry[0], factor[:, 1]) + batch_mm(carry[1], factor[:, 0])
        return ((prod_real, prod_imag), jnp.stack([prod_real, prod_imag], 1))
    start = (jnp.broadcast_to(jnp.eye(NB, dtype=jnp.float32), (NE, NB, NB)), jnp.zeros((NE, NB, NB), jnp.float32))
    final, chained = lax.scan(step, start, factors)
    return (jnp.transpose(lessers, (1, 0, 2, 3, 4)), jnp.transpose(chained, (1, 0, 2, 3, 4)))
```

```python
import functools
import math

import jax
import jax.numpy as jnp
from jax import lax
from jax.experimental import pallas as pl
from jax.experimental.pallas import tpu as pltpu
from jax.sharding import PartitionSpec as P

NB = 64
MODES = 4
KSPAN = 2
ETA = 2.0
BF = jnp.bfloat16
F32 = jnp.float32
MESH = pl.DeviceIdType.MESH


def dot(a, b):
    return jnp.dot(a, b, preferred_element_type=F32)


def dot_t(a, b):
    return lax.dot_general(a, b, (((1,), (1,)), ((), ())), preferred_element_type=F32)


def halves(value):
    high = value.astype(BF)
    return high, (value - high.astype(F32)).astype(BF)


def lane_sign(rows):
    lane = lax.broadcasted_iota(jnp.int32, (rows, 2 * NB), 1)
    return jnp.where(lane < NB, -1.0, 1.0).astype(F32)


def times_i(value):
    return pltpu.roll(value, NB, 1) * lane_sign(value.shape[0])


def eye_pair():
    row = lax.broadcasted_iota(jnp.int32, (NB, 2 * NB), 0)
    lane = lax.broadcasted_iota(jnp.int32, (NB, 2 * NB), 1)
    return jnp.where(row == lane, 1.0, 0.0).astype(F32)


def cmul(a, b):
    full = jnp.concatenate([b, times_i(b)], 0)
    bh, bl = halves(full)
    ah, al = halves(a)
    left = jnp.concatenate([ah, al], 1)
    both = jnp.concatenate([bh, bl], 1)
    right = jnp.concatenate([both, both], 0)
    out = dot(left, right)
    return out[:, : 2 * NB] + out[:, 2 * NB :]


def kernel(
    ng, nx, ny, orb,
    less, ret, ham, coup, occ, shf, face,
    lesser, chain,
    grn, rv, hv, cv, coef, sig, half, new, brow, tcol, facev, pre, outv,
    local_sem, halo_s, halo_r, y_s, y_r, x_s, x_r,
):
    g = lax.axis_index("energy")
    s = lax.axis_index("slab")
    x = lax.div(s, ny)
    y = lax.rem(s, ny)
    slab_y = lambda d: x * ny + lax.rem(y + d + ny, ny)
    slab_x = lambda d: lax.rem(x + d + nx, nx) * ny + y

    own_copy = pltpu.make_async_copy(less.at[:, 0], grn.at[1], local_sem.at[0])
    cv_copy = pltpu.make_async_copy(coup, cv, local_sem.at[1])
    hv_copy = pltpu.make_async_copy(ham.at[0], hv, local_sem.at[2])
    rv_copy = pltpu.make_async_copy(ret.at[:, 0], rv, local_sem.at[3])
    for c in (own_copy, cv_copy, hv_copy, rv_copy):
        c.start()

    barrier = pltpu.get_barrier_semaphore()
    peers = [
        (lax.rem(g + 1, ng), s),
        (lax.rem(g + ng - 1, ng), s),
        (g, slab_y(1)),
        (g, slab_y(-1)),
        (g, slab_x(1)),
        (g, slab_x(-1)),
    ]
    for peer in peers:
        pl.semaphore_signal(barrier, inc=1, device_id=peer, device_id_type=MESH)
    pl.semaphore_wait(barrier, len(peers))

    regions = [
        (pl.ds(0, NB), pl.ds(0, orb)),
        (pl.ds(NB, orb - NB), pl.ds(0, 2 * NB)),
        (pl.ds(NB, orb - NB), pl.ds(2 * NB, orb - 2 * NB)),
    ]

    def halo(side, part):
        rows, cols = regions[part]
        to = lax.rem(g + 1, ng) if side == 0 else lax.rem(g + ng - 1, ng)
        return pltpu.make_async_remote_copy(
            src_ref=less.at[:, 0, :, rows, cols],
            dst_ref=grn.at[0 if side == 0 else 2, :, :, rows, cols],
            send_sem=halo_s.at[side, part],
            recv_sem=halo_r.at[side, part],
            device_id=(to, s),
            device_id_type=MESH,
        )

    for part in range(3):
        @pl.when(g < ng - 1)
        def _():
            halo(0, part).start()

        @pl.when(g > 0)
        def _():
            halo(1, part).start()

    @pl.when(g == 0)
    def _():
        grn[0] = jnp.zeros(grn.shape[1:], BF)

    @pl.when(g == ng - 1)
    def _():
        grn[2] = jnp.zeros(grn.shape[1:], BF)

    cv_copy.wait()
    up_w, low_w = [], []
    for m in range(MODES):
        n = occ[m]
        two = (shf[m] - 1).astype(F32)
        one = 1.0 - two
        up_w.append(((n + 1.0) * one, (n + 1.0) * two))
        low_w.append((n * one, n * two))

    def coef_rows(i, _):
        rows = pl.ds(pl.multiple_of(i * 16, 16), 16)
        planes = [cv[m, rows, :].astype(F32) for m in range(MODES)]
        for k in range(2):
            coef[k, rows, :] = sum(planes[m] * up_w[m][k] for m in range(MODES))
            coef[2 + k, rows, :] = sum(planes[m] * low_w[m][k] for m in range(MODES))
        return 0

    lax.fori_loop(0, orb // 16, coef_rows, 0)

    face_row = jnp.concatenate([face[0].astype(F32), face[1].astype(F32)], 1)
    facev[...] = jnp.concatenate([face_row, times_i(face_row)], 0).astype(BF)

    hv_copy.wait()
    row_i = lax.broadcasted_iota(jnp.int32, (orb, orb), 0)
    col_i = lax.broadcasted_iota(jnp.int32, (orb, orb), 1)
    diag_h = jnp.sum(jnp.where(row_i == col_i, hv[...].astype(F32), 0.0), axis=0, keepdims=True)
    inner = lax.broadcasted_iota(jnp.int32, (1, orb), 1) >= NB
    inverse = []
    for e in range(2):
        energy = -3.0 + 6.0 * ((2 * g + e).astype(F32) + 0.5) * (1.0 / (2 * ng))
        offset = energy - diag_h
        denom = offset * offset + ETA * ETA
        inverse.append((jnp.where(inner, offset / denom, 0.0), jnp.where(inner, -ETA / denom, 0.0)))

    own_copy.wait()

    def halo_wait(part):
        @pl.when(g > 0)
        def _():
            halo(0, part).wait_recv()

        @pl.when(g < ng - 1)
        def _():
            halo(1, part).wait_recv()

    def sigma_region(first, count, cols):
        def body(i, _):
            rows = pl.ds(pl.multiple_of(first + i * 16, 16), 16)
            a1, a2, b1, b2 = [coef[k, rows, cols] for k in range(4)]
            for c in range(2):
                field = [grn[f // 2, f % 2, c, rows, cols].astype(F32) for f in range(6)]
                for e in range(2):
                    total = a1 * field[e + 3] + a2 * field[e + 4] + b1 * field[e + 1] + b2 * field[e]
                    sig[e, c, rows, cols] = total.astype(BF)
            return 0

        lax.fori_loop(0, count // 16, body, 0)

    halo_wait(0)
    sigma_region(0, NB, pl.ds(0, orb))
    halo_wait(1)
    sigma_region(NB, orb - NB, pl.ds(0, 2 * NB))

    lane256 = lax.broadcasted_iota(jnp.int32, (orb, 2 * NB), 1)
    for e in range(2):
        top_r = hv[0:NB, :].astype(F32) + sig[e, 0, 0:NB, :].astype(F32)
        top_i = sig[e, 1, 0:NB, :].astype(F32)
        inv_r, inv_i = inverse[e]
        q_r = (top_r * inv_r - top_i * inv_i).astype(BF)
        q_i = (top_r * inv_i + top_i * inv_r).astype(BF)
        left_r = hv[:, 0 : 2 * NB].astype(F32) + sig[e, 0, :, 0 : 2 * NB].astype(F32)
        left_i = pltpu.roll(sig[e, 1, :, 0 : 2 * NB].astype(F32), NB, 1)
        pair = jnp.where(lane256 < NB, left_r, left_i)
        prod = dot(jnp.concatenate([q_r, q_i], 0), pair.astype(BF))
        bound = pair[0:NB] - (prod[0:NB] + times_i(prod[NB:]))
        brow[y, e] = bound.astype(BF)

    def hop(buf, sems, recvs, e, way, step, n, pos, to):
        idx = lax.rem(pos - (step - 1) + n, n) if way == 0 else lax.rem(pos + (step - 1), n)
        return pltpu.make_async_remote_copy(
            src_ref=buf.at[idx, e],
            dst_ref=buf.at[idx, e],
            send_sem=sems.at[way, step - 1, e],
            recv_sem=recvs.at[way, step - 1, e],
            device_id=(g, to),
            device_id_type=MESH,
        )

    def hop_y(e, way, step):
        return hop(brow, y_s, y_r, e, way, step, ny, y, slab_y(1 if way == 0 else -1))

    def hop_x(e, way, step):
        return hop(tcol, x_s, x_r, e, way, step, nx, x, slab_x(1 if way == 0 else -1))

    def reach(n):
        return n // 2, n // 2 - 1

    def ring(hopper, n, on_arrival, fill):
        ways = reach(n)
        for step in range(1, ways[0] + 1):
            for e in range(2):
                for way in range(2):
                    if step <= ways[way]:
                        hopper(e, way, step).wait_recv()
                        if step < ways[way]:
                            hopper(e, way, step + 1).start()
            for e in range(2):
                for way in range(2):
                    if step <= ways[way]:
                        on_arrival(e, way, step)
            if step < ways[0]:
                fill(step)

    def start_ring(hopper, n, e):
        for way in range(2):
            if reach(n)[way] > 0:
                hopper(e, way, 1).start()

    scale = 1.0 / (8.0 * math.sqrt(NB * nx * ny))

    def factor(idx, e):
        return eye_pair() + scale * dot(brow[idx, e], facev[...])

    for e in range(2):
        start_ring(hop_y, ny, e)

    def rest_of_sigma():
        halo_wait(2)
        sigma_region(NB, orb - NB, pl.ds(2 * NB, orb - 2 * NB))

    def half_block(e):
        rr, ri = rv[e, 0], rv[e, 1]
        sr, si = sig[e, 0], sig[e, 1]
        half[e, 0] = (dot(rr, sr) - dot(ri, si)).astype(BF)
        half[e, 1] = (dot(rr, si) + dot(ri, sr)).astype(BF)

    def new_block(e):
        rr, ri = rv[e, 0], rv[e, 1]
        hr, hi = half[e, 0], half[e, 1]
        new[e, 0] = (dot_t(hr, rr) + dot_t(hi, ri)).astype(BF)
        new[e, 1] = (dot_t(hi, rr) - dot_t(hr, ri)).astype(BF)
        out_copy(e).start()

    def out_copy(e):
        return pltpu.make_async_copy(new.at[e], lesser.at[e, 0], local_sem.at[4 + e])

    rest_of_sigma()
    rv_copy.wait()

    eye = eye_pair()
    prefix = [factor(y, e) for e in range(2)]
    wrapped = [eye, eye]
    suffix_a = [eye, eye]
    suffix_b = [eye, eye]

    def arrive_y(e, way, step):
        if way == 0:
            idx = lax.rem(y - step + ny, ny)
            mine = y - step >= 0
            product = cmul(factor(idx, e), jnp.where(mine, prefix[e], suffix_b[e]))
            prefix[e] = jnp.where(mine, product, prefix[e])
            suffix_b[e] = jnp.where(mine, suffix_b[e], product)
        else:
            idx = lax.rem(y + step, ny)
            after = y + step < ny
            product = cmul(jnp.where(after, suffix_a[e], wrapped[e]), factor(idx, e))
            suffix_a[e] = jnp.where(after, product, suffix_a[e])
            wrapped[e] = jnp.where(after, wrapped[e], product)

    def fill_y(step):
        if step == 1:
            half_block(0)
        elif step == 2:
            half_block(1)

    ring(hop_y, ny, arrive_y, fill_y)
    for e in range(2):
        before = cmul(wrapped[e], prefix[e])
        tcol[x, e] = cmul(before, cmul(suffix_a[e], suffix_b[e]))
        pre[e] = before
        start_ring(hop_x, nx, e)

    if reach(ny)[0] < 3:
        half_block(1)
    if reach(ny)[0] < 2:
        half_block(0)

    total = [pre[0], pre[1]]
    outer = [eye, eye]

    def arrive_x(e, way, step):
        if way == 0:
            idx = lax.rem(x - step + nx, nx)
            block = jnp.where(x - step >= 0, tcol[idx, e], eye)
            total[e] = cmul(block, total[e])
        else:
            idx = lax.rem(x + step, nx)
            block = jnp.where(x + step >= nx, tcol[idx, e], eye)
            outer[e] = cmul(outer[e], block)

    def fill_x(step):
        if step == 1:
            new_block(0)
        elif step == 2:
            new_block(1)

    ring(hop_x, nx, arrive_x, fill_x)
    if reach(nx)[0] < 3:
        new_block(1)
    if reach(nx)[0] < 2:
        new_block(0)

    chain_copies = []
    for e in range(2):
        whole = cmul(outer[e], total[e])
        outv[e, 0] = whole[:, 0:NB]
        outv[e, 1] = pltpu.roll(whole, NB, 1)[:, 0:NB]
        copy = pltpu.make_async_copy(outv.at[e], chain.at[e, 0], local_sem.at[6 + e])
        copy.start()
        chain_copies.append(copy)

    for part in range(3):
        @pl.when(g < ng - 1)
        def _():
            halo(0, part).wait_send()

        @pl.when(g > 0)
        def _():
            halo(1, part).wait_send()

    for hopper, n in ((hop_y, ny), (hop_x, nx)):
        for way in range(2):
            for step in range(1, reach(n)[way] + 1):
                for e in range(2):
                    hopper(e, way, step).wait_send()
    for e in range(2):
        out_copy(e).wait()
        chain_copies[e].wait()


def solution(mesh, grid=None):
    ng, ns = mesh.shape["energy"], mesh.shape["slab"]
    nx, ny = grid or (math.isqrt(ns), ns // math.isqrt(ns))

    def on_device(less, ret, ham, coup, occ, shf, face):
        e_count, orb = less.shape[0], less.shape[3]
        any_space = pl.BlockSpec(memory_space=pl.ANY)
        smem = pl.BlockSpec(memory_space=pltpu.SMEM)
        vmem = pl.BlockSpec(memory_space=pltpu.VMEM)
        reach_y, reach_x = max(ny // 2, 1), max(nx // 2, 1)
        dma = pltpu.SemaphoreType.DMA
        return pl.pallas_call(
            functools.partial(kernel, ng, nx, ny, orb),
            out_shape=(
                jax.ShapeDtypeStruct((e_count, 1, 2, orb, orb), BF),
                jax.ShapeDtypeStruct((e_count, 1, 2, NB, NB), F32),
            ),
            in_specs=[any_space, any_space, any_space, any_space, smem, smem, vmem],
            out_specs=(any_space, any_space),
            scratch_shapes=[
                pltpu.VMEM((3, 2, 2, orb, orb), BF),
                pltpu.VMEM((2, 2, orb, orb), BF),
                pltpu.VMEM((orb, orb), BF),
                pltpu.VMEM((MODES, orb, orb), BF),
                pltpu.VMEM((4, orb, orb), F32),
                pltpu.VMEM((2, 2, orb, orb), BF),
                pltpu.VMEM((2, 2, orb, orb), BF),
                pltpu.VMEM((2, 2, orb, orb), BF),
                pltpu.VMEM((ny, 2, NB, 2 * NB), BF),
                pltpu.VMEM((nx, 2, NB, 2 * NB), F32),
                pltpu.VMEM((2 * NB, 2 * NB), BF),
                pltpu.VMEM((2, NB, 2 * NB), F32),
                pltpu.VMEM((2, 2, NB, NB), F32),
                dma((8,)),
                dma((2, 3)),
                dma((2, 3)),
                dma((2, reach_y, 2)),
                dma((2, reach_y, 2)),
                dma((2, reach_x, 2)),
                dma((2, reach_x, 2)),
            ],
            compiler_params=pltpu.CompilerParams(collective_id=0, has_side_effects=True),
        )(less, ret, ham, coup, occ, shf, face)

    in_specs = (
        P("energy", "slab", None, None, None),
        P("energy", "slab", None, None, None),
        P("slab", None, None),
        P(),
        P(),
        P(),
        P(),
    )
    out_specs = (P("energy", "slab", None, None, None), P("energy", "slab", None, None, None))
    return jax.shard_map(on_device, mesh=mesh, in_specs=in_specs, out_specs=out_specs, check_vma=False)
```

```python
import functools
import math

import jax
import jax.numpy as jnp
from jax import lax
from jax.experimental import pallas as pl
from jax.experimental.pallas import tpu as pltpu
from jax.sharding import PartitionSpec as P

NB = 64
MODES = 4
KSPAN = 2
ETA = 2.0
BF = jnp.bfloat16
F32 = jnp.float32
MESH = pl.DeviceIdType.MESH


def dot(a, b):
    return jnp.dot(a, b, preferred_element_type=F32)


def dot_t(a, b):
    return lax.dot_general(a, b, (((1,), (1,)), ((), ())), preferred_element_type=F32)


def halves(value):
    high = value.astype(BF)
    return high, (value - high.astype(F32)).astype(BF)


def lane_sign(rows):
    lane = lax.broadcasted_iota(jnp.int32, (rows, 2 * NB), 1)
    return jnp.where(lane < NB, -1.0, 1.0).astype(F32)


def times_i(value):
    return pltpu.roll(value, NB, 1) * lane_sign(value.shape[0])


def eye_pair():
    row = lax.broadcasted_iota(jnp.int32, (NB, 2 * NB), 0)
    lane = lax.broadcasted_iota(jnp.int32, (NB, 2 * NB), 1)
    return jnp.where(row == lane, 1.0, 0.0).astype(F32)


def cmul(a, b):
    full = jnp.concatenate([b, times_i(b)], 0)
    bh, bl = halves(full)
    ah, al = halves(a)
    left = jnp.concatenate([ah, al], 1)
    both = jnp.concatenate([bh, bl], 1)
    right = jnp.concatenate([both, both], 0)
    out = dot(left, right)
    return out[:, : 2 * NB] + out[:, 2 * NB :]


def kernel(
    ng, nx, ny, orb,
    less, ret, ham, coup, occ, shf, face,
    lesser, chain,
    grn, rv, hv, cv, coef, sig, half, brow, tcol, facev, pre, swap,
    local_sem, ready, halo_s, halo_r, y_s, y_r, x_s, x_r, swap_s, swap_r,
):
    g = lax.axis_index("energy")
    s = lax.axis_index("slab")
    x = lax.div(s, ny)
    y = lax.rem(s, ny)
    slab_y = lambda d: x * ny + lax.rem(y + d + ny, ny)
    slab_x = lambda d: lax.rem(x + d + nx, nx) * ny + y
    mine = lax.rem(y, 2)
    other = 1 - mine

    own_copy = pltpu.make_async_copy(less.at[:, 0], grn.at[1], local_sem.at[0])
    cv_copy = pltpu.make_async_copy(coup, cv, local_sem.at[1])
    hv_copy = pltpu.make_async_copy(ham.at[0], hv, local_sem.at[2])
    rv_copy = pltpu.make_async_copy(ret.at[:, 0], rv, local_sem.at[3])
    for c in (cv_copy, own_copy, hv_copy, rv_copy):
        c.start()

    barrier = pltpu.get_barrier_semaphore()
    around = [slab_y(1), slab_y(-1), slab_x(1), slab_x(-1)]
    peers = [(lax.rem(g + 1, ng), s), (lax.rem(g + ng - 1, ng), s)] + [(g, p) for p in around]
    for peer in peers:
        pl.semaphore_signal(barrier, inc=1, device_id=peer, device_id_type=MESH)
    pl.semaphore_wait(barrier, len(peers))

    last_round = max(nx, ny) // 2

    def tell(r):
        if 2 <= r <= last_round:
            for way, p in enumerate(around):
                pl.semaphore_signal(ready.at[way, r - 2], inc=1, device_id=(g, p), device_id_type=MESH)

    def hear(r):
        if 2 <= r <= last_round:
            for way in range(4):
                pl.semaphore_wait(ready.at[way, r - 2], 1)

    regions = [
        (pl.ds(0, NB), pl.ds(0, orb)),
        (pl.ds(NB, orb - NB), pl.ds(0, 2 * NB)),
        (pl.ds(NB, orb - NB), pl.ds(2 * NB, orb - 2 * NB)),
    ]

    def halo(side, part):
        rows, cols = regions[part]
        to = lax.rem(g + 1, ng) if side == 0 else lax.rem(g + ng - 1, ng)
        return pltpu.make_async_remote_copy(
            src_ref=less.at[:, 0, :, rows, cols],
            dst_ref=grn.at[0 if side == 0 else 2, :, :, rows, cols],
            send_sem=halo_s.at[side, part],
            recv_sem=halo_r.at[side, part],
            device_id=(to, s),
            device_id_type=MESH,
        )

    for part in range(3):
        @pl.when(g < ng - 1)
        def _():
            halo(0, part).start()

        @pl.when(g > 0)
        def _():
            halo(1, part).start()

    tell(2)

    @pl.when(g == 0)
    def _():
        grn[0] = jnp.zeros(grn.shape[1:], BF)

    @pl.when(g == ng - 1)
    def _():
        grn[2] = jnp.zeros(grn.shape[1:], BF)

    cv_copy.wait()
    up_w, low_w = [], []
    for m in range(MODES):
        n = occ[m]
        two = (shf[m] - 1).astype(F32)
        one = 1.0 - two
        up_w.append(((n + 1.0) * one, (n + 1.0) * two))
        low_w.append((n * one, n * two))

    def coef_rows(i, _):
        rows = pl.ds(pl.multiple_of(i * 16, 16), 16)
        planes = [cv[m, rows, :].astype(F32) for m in range(MODES)]
        for k in range(2):
            coef[k, rows, :] = sum(planes[m] * up_w[m][k] for m in range(MODES))
            coef[2 + k, rows, :] = sum(planes[m] * low_w[m][k] for m in range(MODES))
        return 0

    lax.fori_loop(0, orb // 16, coef_rows, 0)
    hear(2)
    tell(3)

    face_row = jnp.concatenate([face[0].astype(F32), face[1].astype(F32)], 1)
    facev[...] = jnp.concatenate([face_row, times_i(face_row)], 0).astype(BF)

    hv_copy.wait()
    row_i = lax.broadcasted_iota(jnp.int32, (orb, orb), 0)
    col_i = lax.broadcasted_iota(jnp.int32, (orb, orb), 1)
    diag_h = jnp.sum(jnp.where(row_i == col_i, hv[...].astype(F32), 0.0), axis=0, keepdims=True)
    inner = lax.broadcasted_iota(jnp.int32, (1, orb), 1) >= NB
    inverse = []
    for e in range(2):
        energy = -3.0 + 6.0 * ((2 * g + e).astype(F32) + 0.5) * (1.0 / (2 * ng))
        offset = energy - diag_h
        denom = offset * offset + ETA * ETA
        inverse.append((jnp.where(inner, offset / denom, 0.0), jnp.where(inner, -ETA / denom, 0.0)))

    own_copy.wait()
    hear(3)
    tell(4)

    def halo_wait(part):
        @pl.when(g > 0)
        def _():
            halo(0, part).wait_recv()

        @pl.when(g < ng - 1)
        def _():
            halo(1, part).wait_recv()

    def sigma_region(first, count, cols):
        def body(i, _):
            rows = pl.ds(pl.multiple_of(first + i * 16, 16), 16)
            a1, a2, b1, b2 = [coef[k, rows, cols] for k in range(4)]
            for c in range(2):
                field = [grn[f // 2, f % 2, c, rows, cols].astype(F32) for f in range(6)]
                for e in range(2):
                    total = a1 * field[e + 3] + a2 * field[e + 4] + b1 * field[e + 1] + b2 * field[e]
                    sig[e, c, rows, cols] = total.astype(BF)
            return 0

        lax.fori_loop(0, count // 16, body, 0)

    halo_wait(0)
    sigma_region(0, NB, pl.ds(0, orb))
    halo_wait(1)
    sigma_region(NB, orb - NB, pl.ds(0, 2 * NB))

    lane256 = lax.broadcasted_iota(jnp.int32, (orb, 2 * NB), 1)
    for e in range(2):
        top_r = hv[0:NB, :].astype(F32) + sig[e, 0, 0:NB, :].astype(F32)
        top_i = sig[e, 1, 0:NB, :].astype(F32)
        inv_r, inv_i = inverse[e]
        q_r = (top_r * inv_r - top_i * inv_i).astype(BF)
        q_i = (top_r * inv_i + top_i * inv_r).astype(BF)
        left_r = hv[:, 0 : 2 * NB].astype(F32) + sig[e, 0, :, 0 : 2 * NB].astype(F32)
        left_i = pltpu.roll(sig[e, 1, :, 0 : 2 * NB].astype(F32), NB, 1)
        pair = jnp.where(lane256 < NB, left_r, left_i)
        prod = dot(jnp.concatenate([q_r, q_i], 0), pair.astype(BF))
        bound = pair[0:NB] - (prod[0:NB] + times_i(prod[NB:]))
        brow[e, y] = bound.astype(BF)

    for r in range(4, last_round + 1):
        hear(r)
        tell(r + 1)

    far_first = lambda n: sorted(range(1, n), key=lambda d: -min(d, n - d))

    def row_send(d, first):
        to = lax.rem(y + d, ny)
        e = lax.rem(to, 2) if first else 1 - lax.rem(to, 2)
        return pltpu.make_async_remote_copy(
            src_ref=brow.at[e, y],
            dst_ref=brow.at[e, y],
            send_sem=y_s.at[0 if first else 1, d - 1],
            recv_sem=y_r.at[0 if first else 1, y],
            device_id=(g, slab_y(d)),
            device_id_type=MESH,
        )

    def row_wait(source, first):
        e = mine if first else other
        pltpu.make_async_remote_copy(
            src_ref=brow.at[e, source],
            dst_ref=brow.at[e, source],
            send_sem=y_s.at[0 if first else 1, 0],
            recv_sem=y_r.at[0 if first else 1, source],
            device_id=(g, slab_y(1)),
            device_id_type=MESH,
        ).wait_recv()

    for d in far_first(ny):
        row_send(d, True).start()
    for d in far_first(ny):
        @pl.when(y + d < ny)
        def _():
            row_send(d, False).start()

    halo_wait(2)
    sigma_region(NB, orb - NB, pl.ds(2 * NB, orb - 2 * NB))
    rv_copy.wait()
    for e in range(2):
        rr, ri = rv[e, 0], rv[e, 1]
        sr, si = sig[e, 0], sig[e, 1]
        half[e, 0] = (dot(rr, sr) - dot(ri, si)).astype(BF)
        half[e, 1] = (dot(rr, si) + dot(ri, sr)).astype(BF)
    for e in range(2):
        rr, ri = rv[e, 0], rv[e, 1]
        hr, hi = half[e, 0], half[e, 1]
        lesser[e, 0, 0] = (dot_t(hr, rr) + dot_t(hi, ri)).astype(BF)
        lesser[e, 0, 1] = (dot_t(hi, rr) - dot_t(hr, ri)).astype(BF)

    scale = 1.0 / (8.0 * math.sqrt(NB * nx * ny))
    eye = eye_pair()

    def factors(e):
        rows = dot(brow[e].reshape(ny * NB, 2 * NB), facev[...])
        return [eye + scale * rows[i * NB : (i + 1) * NB] for i in range(ny)]

    def ordered_product(blocks):
        while len(blocks) > 1:
            pairs = [cmul(blocks[i], blocks[i + 1]) for i in range(0, len(blocks) - 1, 2)]
            blocks = pairs + blocks[len(blocks) - len(blocks) % 2 :]
        return blocks[0]

    for d in range(1, ny):
        row_wait(lax.rem(y + d, ny), True)
    tcol[x] = ordered_product(factors(mine))

    def total_send(d):
        return pltpu.make_async_remote_copy(
            src_ref=tcol.at[x],
            dst_ref=tcol.at[x],
            send_sem=x_s.at[d - 1],
            recv_sem=x_r.at[x],
            device_id=(g, slab_x(d)),
            device_id_type=MESH,
        )

    for d in far_first(nx):
        @pl.when(x + d < nx)
        def _():
            total_send(d).start()

    for d in range(1, ny):
        @pl.when(y - d >= 0)
        def _():
            row_wait(lax.rem(y - d + ny, ny), False)
    for e in range(2):
        pre[e] = ordered_product([jnp.where(i <= y, f, eye) for i, f in enumerate(factors(e))])

    for d in range(1, nx):
        @pl.when(x - d >= 0)
        def _():
            source = lax.rem(x - d + nx, nx)
            pltpu.make_async_remote_copy(
                src_ref=tcol.at[source],
                dst_ref=tcol.at[source],
                send_sem=x_s.at[0],
                recv_sem=x_r.at[source],
                device_id=(g, slab_x(1)),
                device_id_type=MESH,
            ).wait_recv()
    swap[0] = ordered_product([jnp.where(i < x, tcol[i], eye) for i in range(nx - 1)])
    swap_copy = pltpu.make_async_remote_copy(
        src_ref=swap.at[0],
        dst_ref=swap.at[1],
        send_sem=swap_s.at[0],
        recv_sem=swap_r.at[0],
        device_id=(g, slab_y(1 - 2 * mine)),
        device_id_type=MESH,
    )
    swap_copy.start()

    def finish(e, rows_before):
        whole = cmul(rows_before, pre[e])
        chain[e, 0, 0] = whole[:, 0:NB]
        chain[e, 0, 1] = pltpu.roll(whole, NB, 1)[:, 0:NB]

    finish(mine, swap[0])

    for part in range(3):
        @pl.when(g < ng - 1)
        def _():
            halo(0, part).wait_send()

        @pl.when(g > 0)
        def _():
            halo(1, part).wait_send()

    for d in range(1, ny):
        row_send(d, True).wait_send()

        @pl.when(y + d < ny)
        def _():
            row_send(d, False).wait_send()

    for d in range(1, nx):
        @pl.when(x + d < nx)
        def _():
            total_send(d).wait_send()

    swap_copy.wait()
    finish(other, swap[1])


def solution(mesh, grid=None):
    ng, ns = mesh.shape["energy"], mesh.shape["slab"]
    nx, ny = grid or (math.isqrt(ns), ns // math.isqrt(ns))

    def on_device(less, ret, ham, coup, occ, shf, face):
        e_count, orb = less.shape[0], less.shape[3]
        any_space = pl.BlockSpec(memory_space=pl.ANY)
        smem = pl.BlockSpec(memory_space=pltpu.SMEM)
        vmem = pl.BlockSpec(memory_space=pltpu.VMEM)
        dma = pltpu.SemaphoreType.DMA
        rounds = max(max(nx, ny) // 2 - 1, 1)
        return pl.pallas_call(
            functools.partial(kernel, ng, nx, ny, orb),
            out_shape=(
                pltpu.VMEM((e_count, 1, 2, orb, orb), BF),
                pltpu.VMEM((e_count, 1, 2, NB, NB), F32),
            ),
            in_specs=[any_space, any_space, any_space, any_space, smem, smem, vmem],
            out_specs=(vmem, vmem),
            scratch_shapes=[
                pltpu.VMEM((3, 2, 2, orb, orb), BF),
                pltpu.VMEM((2, 2, orb, orb), BF),
                pltpu.VMEM((orb, orb), BF),
                pltpu.VMEM((MODES, orb, orb), BF),
                pltpu.VMEM((4, orb, orb), F32),
                pltpu.VMEM((2, 2, orb, orb), BF),
                pltpu.VMEM((2, 2, orb, orb), BF),
                pltpu.VMEM((2, ny, NB, 2 * NB), BF),
                pltpu.VMEM((nx, NB, 2 * NB), F32),
                pltpu.VMEM((2 * NB, 2 * NB), BF),
                pltpu.VMEM((2, NB, 2 * NB), F32),
                pltpu.VMEM((2, NB, 2 * NB), F32),
                dma((4,)),
                pltpu.SemaphoreType.REGULAR((4, rounds)),
                dma((2, 3)),
                dma((2, 3)),
                dma((2, ny - 1)),
                dma((2, ny)),
                dma((nx - 1,)),
                dma((nx,)),
                dma((1,)),
                dma((1,)),
            ],
            compiler_params=pltpu.CompilerParams(collective_id=0, has_side_effects=True),
        )(less, ret, ham, coup, occ, shf, face)

    in_specs = (
        P("energy", "slab", None, None, None),
        P("energy", "slab", None, None, None),
        P("slab", None, None),
        P(),
        P(),
        P(),
        P(),
    )
    out_specs = (P("energy", "slab", None, None, None), P("energy", "slab", None, None, None))
    return jax.shard_map(on_device, mesh=mesh, in_specs=in_specs, out_specs=out_specs, check_vma=False)
```

```python
import functools
import math

import jax
import jax.numpy as jnp
from jax import lax
from jax.experimental import pallas as pl
from jax.experimental.pallas import tpu as pltpu
from jax.sharding import PartitionSpec as P

NB = 64
MODES = 4
KSPAN = 2
ETA = 2.0
LATE = 2
BF = jnp.bfloat16
F32 = jnp.float32
MESH = pl.DeviceIdType.MESH


def dot(a, b):
    return jnp.dot(a, b, preferred_element_type=F32)


def dot_t(a, b):
    return lax.dot_general(a, b, (((1,), (1,)), ((), ())), preferred_element_type=F32)


def halves(value):
    high = value.astype(BF)
    return high, (value - high.astype(F32)).astype(BF)


def lane_sign(rows):
    lane = lax.broadcasted_iota(jnp.int32, (rows, 2 * NB), 1)
    return jnp.where(lane < NB, -1.0, 1.0).astype(F32)


def times_i(value):
    return pltpu.roll(value, NB, 1) * lane_sign(value.shape[0])


def eye_pair():
    row = lax.broadcasted_iota(jnp.int32, (NB, 2 * NB), 0)
    lane = lax.broadcasted_iota(jnp.int32, (NB, 2 * NB), 1)
    return jnp.where(row == lane, 1.0, 0.0).astype(F32)


def cmul(a, b):
    full = jnp.concatenate([b, times_i(b)], 0)
    bh, bl = halves(full)
    ah, al = halves(a)
    left = jnp.concatenate([ah, al], 1)
    both = jnp.concatenate([bh, bl], 1)
    right = jnp.concatenate([both, both], 0)
    out = dot(left, right)
    return out[:, : 2 * NB] + out[:, 2 * NB :]


def kernel(
    ng, nx, ny, orb,
    less, ret, ham, coup, occ, shf, face,
    lesser, chain,
    grn, rv, hv, cv, coef, sig, half, brow, tcol, facev, pre, before, first_b,
    local_sem, ready, hello, halo_s, halo_r, y_s, y_r, x_s, x_r, swap_s, swap_r, first_s, first_r,
):
    g = lax.axis_index("energy")
    s = lax.axis_index("slab")
    x = lax.div(s, ny)
    y = lax.rem(s, ny)
    slab_y = lambda d: x * ny + lax.rem(y + d + ny, ny)
    slab_x = lambda d: lax.rem(x + d + nx, nx) * ny + y
    mine = lax.rem(y, 2)
    other = 1 - mine

    own_copy = pltpu.make_async_copy(less.at[:, 0], grn.at[1], local_sem.at[0])
    cv_copy = pltpu.make_async_copy(coup, cv, local_sem.at[1])
    hv_copy = pltpu.make_async_copy(ham.at[0], hv, local_sem.at[2])
    rv_copy = pltpu.make_async_copy(ret.at[:, 0], rv, local_sem.at[3])
    for c in (cv_copy, own_copy, hv_copy, rv_copy):
        c.start()

    late = g < LATE
    slab0 = s == 0
    late0 = late & slab0
    device0 = (g == 0) & slab0
    line_y = late & (x == 0)
    line_x = late & (y == 0)

    barrier = pltpu.get_barrier_semaphore()

    def greet(to, cond):
        @pl.when(cond)
        def _():
            pl.semaphore_signal(barrier, inc=1, device_id=to, device_id_type=MESH)

    around = [slab_y(1), slab_y(-1), slab_x(1), slab_x(-1)]
    up_g, down_g = jnp.minimum(g + 1, ng - 1), jnp.maximum(g - 1, 0)
    greet((up_g, s), (g < ng - 1) & jnp.logical_not(device0))
    greet((down_g, s), g > 0)
    for p in around:
        greet((g, p), jnp.logical_not(late0))
    greet((g, 0), (line_y & (y > 1) & (y < ny - 1)) | (line_x & (x > 1) & (x < nx - 1)))
    awaited = (g < ng - 1).astype(jnp.int32) + ((g > 0) & jnp.logical_not((g == 1) & slab0)).astype(jnp.int32)
    for p in around:
        awaited = awaited + jnp.logical_not(late & (p == 0)).astype(jnp.int32)
    awaited = awaited + jnp.where(late0, ny + nx - 6, 0)
    pl.semaphore_wait(barrier, awaited)

    @pl.when(device0)
    def _():
        pl.semaphore_signal(hello.at[0], inc=1, device_id=(up_g, s), device_id_type=MESH)

    def chain_rounds(axis):
        p, n, line = (y, ny, line_y) if axis == 0 else (x, nx, line_x)

        def known(q, r, up):
            on_line = (q - r >= 1) if up else (q + r <= n - 1)
            return jnp.where(line, on_line & (q > 0), r <= n // 2)

        def tell(r):
            for way, up in ((0, True), (1, False)):
                q = lax.rem(p + (1 if up else n - 1), n)
                good = known(q, r, up) & jnp.logical_not(line & (p == 0))

                @pl.when(good)
                def _():
                    to = around[2 * axis + way]
                    pl.semaphore_signal(ready.at[2 * axis + way, r - 2], inc=1, device_id=(g, to), device_id_type=MESH)

        def hear(r, cond):
            for way, up in ((0, True), (1, False)):
                @pl.when(known(p, r, up) & cond)
                def _():
                    pl.semaphore_wait(ready.at[2 * axis + way, r - 2], 1)

        return tell, hear

    tell_y, hear_y = chain_rounds(0)
    tell_x, hear_x = chain_rounds(1)
    always = s >= 0
    last_y, last_x = max(ny - 2, 1), max(nx - 2, 1)

    regions = [
        (pl.ds(0, NB), pl.ds(0, orb)),
        (pl.ds(NB, orb - NB), pl.ds(0, 2 * NB)),
        (pl.ds(NB, orb - NB), pl.ds(2 * NB, orb - 2 * NB)),
    ]

    def halo(side, part):
        rows, cols = regions[part]
        to = lax.rem(g + 1, ng) if side == 0 else lax.rem(g + ng - 1, ng)
        return pltpu.make_async_remote_copy(
            src_ref=less.at[:, 0, :, rows, cols],
            dst_ref=grn.at[0 if side == 0 else 2, :, :, rows, cols],
            send_sem=halo_s.at[side, part],
            recv_sem=halo_r.at[side, part],
            device_id=(to, s),
            device_id_type=MESH,
        )

    for part in range(3):
        @pl.when(g < ng - 1)
        def _():
            halo(0, part).start()

        @pl.when((g > 0) & jnp.logical_not((g == 1) & slab0))
        def _():
            halo(1, part).start()

    if last_y >= 2:
        tell_y(2)
    if last_x >= 2:
        tell_x(2)

    @pl.when((g == 1) & slab0)
    def _():
        pl.semaphore_wait(hello.at[0], 1)
        for part in range(3):
            halo(1, part).start()

    @pl.when(g == 0)
    def _():
        grn[0] = jnp.zeros(grn.shape[1:], BF)

    @pl.when(g == ng - 1)
    def _():
        grn[2] = jnp.zeros(grn.shape[1:], BF)

    cv_copy.wait()
    up_w, low_w = [], []
    for m in range(MODES):
        n = occ[m]
        two = (shf[m] - 1).astype(F32)
        one = 1.0 - two
        up_w.append(((n + 1.0) * one, (n + 1.0) * two))
        low_w.append((n * one, n * two))

    def coef_rows(i, _):
        rows = pl.ds(pl.multiple_of(i * 16, 16), 16)
        planes = [cv[m, rows, :].astype(F32) for m in range(MODES)]
        for k in range(2):
            coef[k, rows, :] = sum(planes[m] * up_w[m][k] for m in range(MODES))
            coef[2 + k, rows, :] = sum(planes[m] * low_w[m][k] for m in range(MODES))
        return 0

    lax.fori_loop(0, orb // 16, coef_rows, 0)
    def round_y(r):
        if r <= last_y:
            hear_y(r, always)
        if r + 1 <= last_y:
            tell_y(r + 1)

    round_y(2)

    face_row = jnp.concatenate([face[0].astype(F32), face[1].astype(F32)], 1)
    facev[...] = jnp.concatenate([face_row, times_i(face_row)], 0).astype(BF)

    hv_copy.wait()
    row_i = lax.broadcasted_iota(jnp.int32, (orb, orb), 0)
    col_i = lax.broadcasted_iota(jnp.int32, (orb, orb), 1)
    diag_h = jnp.sum(jnp.where(row_i == col_i, hv[...].astype(F32), 0.0), axis=0, keepdims=True)
    inner = lax.broadcasted_iota(jnp.int32, (1, orb), 1) >= NB
    inverse = []
    for e in range(2):
        energy = -3.0 + 6.0 * ((2 * g + e).astype(F32) + 0.5) * (1.0 / (2 * ng))
        offset = energy - diag_h
        denom = offset * offset + ETA * ETA
        inverse.append((jnp.where(inner, offset / denom, 0.0), jnp.where(inner, -ETA / denom, 0.0)))

    own_copy.wait()
    round_y(3)

    def halo_wait(part):
        @pl.when(g > 0)
        def _():
            halo(0, part).wait_recv()

        @pl.when(g < ng - 1)
        def _():
            halo(1, part).wait_recv()

    def sigma_region(first, count, cols):
        def body(i, _):
            rows = pl.ds(pl.multiple_of(first + i * 16, 16), 16)
            a1, a2, b1, b2 = [coef[k, rows, cols] for k in range(4)]
            for c in range(2):
                field = [grn[f // 2, f % 2, c, rows, cols].astype(F32) for f in range(6)]
                for e in range(2):
                    total = a1 * field[e + 3] + a2 * field[e + 4] + b1 * field[e + 1] + b2 * field[e]
                    sig[e, c, rows, cols] = total.astype(BF)
            return 0

        lax.fori_loop(0, count // 16, body, 0)

    halo_wait(0)
    sigma_region(0, NB, pl.ds(0, orb))
    halo_wait(1)
    sigma_region(NB, orb - NB, pl.ds(0, 2 * NB))

    lane256 = lax.broadcasted_iota(jnp.int32, (orb, 2 * NB), 1)
    for e in range(2):
        top_r = hv[0:NB, :].astype(F32) + sig[e, 0, 0:NB, :].astype(F32)
        top_i = sig[e, 1, 0:NB, :].astype(F32)
        inv_r, inv_i = inverse[e]
        q_r = (top_r * inv_r - top_i * inv_i).astype(BF)
        q_i = (top_r * inv_i + top_i * inv_r).astype(BF)
        left_r = hv[:, 0 : 2 * NB].astype(F32) + sig[e, 0, :, 0 : 2 * NB].astype(F32)
        left_i = pltpu.roll(sig[e, 1, :, 0 : 2 * NB].astype(F32), NB, 1)
        pair = jnp.where(lane256 < NB, left_r, left_i)
        prod = dot(jnp.concatenate([q_r, q_i], 0), pair.astype(BF))
        bound = pair[0:NB] - (prod[0:NB] + times_i(prod[NB:]))
        brow[e, y] = bound.astype(BF)

    for r in range(4, last_y + 1):
        round_y(r)

    def first_send(k):
        to = slab_x(k + 1) if k < nx - 1 else slab_y(k - nx + 2)
        return pltpu.make_async_remote_copy(
            src_ref=brow.at[:, 0],
            dst_ref=first_b,
            send_sem=first_s.at[k],
            recv_sem=first_r.at[0],
            device_id=(g, to),
            device_id_type=MESH,
        )

    def first_pass(d):
        return pltpu.make_async_remote_copy(
            src_ref=first_b,
            dst_ref=first_b,
            send_sem=first_s.at[d - 1],
            recv_sem=first_r.at[0],
            device_id=(g, slab_y(d)),
            device_id_type=MESH,
        )

    @pl.when(late0)
    def _():
        for k in sorted(range(nx - 1), key=lambda k: -min(k + 1, nx - 1 - k)):
            first_send(k).start()
        for k in range(nx - 1, nx + ny - 2):
            first_send(k).start()
        first_b[...] = brow[:, 0]

    far_first = lambda n: sorted(range(1, n), key=lambda d: -min(d, n - d))

    def row_send(d, first):
        to = lax.rem(y + d, ny)
        e = lax.rem(to, 2) if first else 1 - lax.rem(to, 2)
        return pltpu.make_async_remote_copy(
            src_ref=brow.at[e, y],
            dst_ref=brow.at[e, y],
            send_sem=y_s.at[0 if first else 1, d - 1],
            recv_sem=y_r.at[0 if first else 1, y],
            device_id=(g, slab_y(d)),
            device_id_type=MESH,
        )

    def row_wait(source, first):
        e = mine if first else other
        pltpu.make_async_remote_copy(
            src_ref=brow.at[e, source],
            dst_ref=brow.at[e, source],
            send_sem=y_s.at[0 if first else 1, 0],
            recv_sem=y_r.at[0 if first else 1, source],
            device_id=(g, slab_y(1)),
            device_id_type=MESH,
        ).wait_recv()

    def sends_first(d):
        return jnp.logical_not(late0 | (late & (lax.rem(y + d, ny) == 0)))

    def sends_second(d):
        return (y + d < ny) & jnp.logical_not(late0)

    for d in far_first(ny):
        @pl.when(sends_first(d))
        def _():
            row_send(d, True).start()

    for d in far_first(ny):
        @pl.when(sends_second(d))
        def _():
            row_send(d, False).start()

    def round_x(r):
        if r <= last_x:
            hear_x(r, jnp.logical_not(late0))
        if r + 1 <= last_x:
            tell_x(r + 1)

    round_x(2)
    halo_wait(2)
    sigma_region(NB, orb - NB, pl.ds(2 * NB, orb - 2 * NB))
    round_x(3)
    rv_copy.wait()
    for e in range(2):
        rr, ri = rv[e, 0], rv[e, 1]
        sr, si = sig[e, 0], sig[e, 1]
        half[e, 0] = (dot(rr, sr) - dot(ri, si)).astype(BF)
        half[e, 1] = (dot(rr, si) + dot(ri, sr)).astype(BF)
    for e in range(2):
        rr, ri = rv[e, 0], rv[e, 1]
        hr, hi = half[e, 0], half[e, 1]
        lesser[e, 0, 0] = (dot_t(hr, rr) + dot_t(hi, ri)).astype(BF)
        lesser[e, 0, 1] = (dot_t(hi, rr) - dot_t(hr, ri)).astype(BF)

    for r in range(4, last_x + 1):
        round_x(r)

    scale = 1.0 / (8.0 * math.sqrt(NB * nx * ny))
    eye = eye_pair()

    def factors(e):
        rows = dot(brow[e].reshape(ny * NB, 2 * NB), facev[...])
        return [eye + scale * rows[i * NB : (i + 1) * NB] for i in range(ny)]

    def ordered_product(blocks):
        while len(blocks) > 1:
            pairs = [cmul(blocks[i], blocks[i + 1]) for i in range(0, len(blocks) - 1, 2)]
            blocks = pairs + blocks[len(blocks) - len(blocks) % 2 :]
        return blocks[0]

    def used(i):
        return jnp.logical_not(line_y) if i == 0 else always

    for d in range(1, ny):
        source = lax.rem(y + d, ny)

        @pl.when(jnp.logical_not(line_x | (line_y & (source == 0))))
        def _():
            row_wait(source, True)

    tcol[x] = ordered_product([jnp.where(used(i), f, eye) for i, f in enumerate(factors(mine))])

    def total_send(d):
        return pltpu.make_async_remote_copy(
            src_ref=tcol.at[x],
            dst_ref=tcol.at[x],
            send_sem=x_s.at[d - 1],
            recv_sem=x_r.at[x],
            device_id=(g, slab_x(d)),
            device_id_type=MESH,
        )

    def sends_total(d):
        return (x + d < nx) & jnp.logical_not(line_x)

    for d in far_first(nx):
        @pl.when(sends_total(d))
        def _():
            total_send(d).start()

    for d in range(1, ny):
        @pl.when((y - d >= 0) & jnp.logical_not(line_y & (y == d)))
        def _():
            row_wait(lax.rem(y - d + ny, ny), False)
    for e in range(2):
        pre[e] = ordered_product([jnp.where((i <= y) & used(i), f, eye) for i, f in enumerate(factors(e))])

    def first_wait():
        pltpu.make_async_remote_copy(
            src_ref=first_b,
            dst_ref=first_b,
            send_sem=first_s.at[0],
            recv_sem=first_r.at[0],
            device_id=(g, slab_y(1)),
            device_id_type=MESH,
        ).wait_recv()

    passing = line_x & (x > 0)

    @pl.when(passing)
    def _():
        first_wait()
        for d in far_first(ny):
            first_pass(d).start()

    for d in range(1, nx):
        @pl.when((x - d >= 0) & jnp.logical_not(line_x))
        def _():
            source = lax.rem(x - d + nx, nx)
            pltpu.make_async_remote_copy(
                src_ref=tcol.at[source],
                dst_ref=tcol.at[source],
                send_sem=x_s.at[0],
                recv_sem=x_r.at[source],
                device_id=(g, slab_x(1)),
                device_id_type=MESH,
            ).wait_recv()

    def swap_copy(k):
        to = slab_y(1 - 2 * mine) if k == 0 else slab_y(-k)
        return pltpu.make_async_remote_copy(
            src_ref=before.at[mine],
            dst_ref=before.at[mine],
            send_sem=swap_s.at[k],
            recv_sem=swap_r.at[mine],
            device_id=(g, to),
            device_id_type=MESH,
        )

    swaps = [
        (x > 0) & jnp.logical_not(line_x),
        (x > 0) & late & (y == 2),
        (x > 0) & late & (y == 2),
    ]
    rows_before = ordered_product([jnp.where(i < x, tcol[i], eye) for i in range(nx - 1)])

    @pl.when(jnp.logical_not(line_x))
    def _():
        before[mine] = rows_before

    for k in range(3):
        @pl.when(swaps[k])
        def _():
            swap_copy(k).start()

    def before_wait(e):
        pltpu.make_async_remote_copy(
            src_ref=before.at[e],
            dst_ref=before.at[e],
            send_sem=swap_s.at[0],
            recv_sem=swap_r.at[e],
            device_id=(g, slab_y(1)),
            device_id_type=MESH,
        ).wait_recv()

    def inner_part(e):
        pre[e] = cmul(jnp.where(x > 0, before[e], eye), pre[e])

    def store(e, whole):
        chain[e, 0, 0] = whole[:, 0:NB]
        chain[e, 0, 1] = pltpu.roll(whole, NB, 1)[:, 0:NB]

    @pl.when((x > 0) & line_x)
    def _():
        before_wait(mine)

    inner_part(mine)

    for part in range(3):
        @pl.when(g < ng - 1)
        def _():
            halo(0, part).wait_send()

        @pl.when(g > 0)
        def _():
            halo(1, part).wait_send()

    for d in range(1, ny):
        @pl.when(sends_first(d))
        def _():
            row_send(d, True).wait_send()

        @pl.when(sends_second(d))
        def _():
            row_send(d, False).wait_send()

        @pl.when(passing)
        def _():
            first_pass(d).wait_send()

    for d in range(1, nx):
        @pl.when(sends_total(d))
        def _():
            total_send(d).wait_send()

    @pl.when(x > 0)
    def _():
        before_wait(other)

    inner_part(other)

    @pl.when(late & jnp.logical_not(slab0 | passing))
    def _():
        first_wait()

    @pl.when(late)
    def _():
        for e in range(2):
            store(e, cmul(eye + scale * dot(first_b[e], facev[...]), pre[e]))

    @pl.when(jnp.logical_not(late))
    def _():
        for e in range(2):
            store(e, pre[e])

    for k in range(3):
        @pl.when(swaps[k])
        def _():
            swap_copy(k).wait_send()

    @pl.when(late0)
    def _():
        for k in range(nx + ny - 2):
            first_send(k).wait_send()


def solution(mesh, grid=None):
    ng, ns = mesh.shape["energy"], mesh.shape["slab"]
    nx, ny = grid or (math.isqrt(ns), ns // math.isqrt(ns))

    def on_device(less, ret, ham, coup, occ, shf, face):
        e_count, orb = less.shape[0], less.shape[3]
        any_space = pl.BlockSpec(memory_space=pl.ANY)
        smem = pl.BlockSpec(memory_space=pltpu.SMEM)
        vmem = pl.BlockSpec(memory_space=pltpu.VMEM)
        dma = pltpu.SemaphoreType.DMA
        rounds = max(max(nx, ny) - 3, 1)
        return pl.pallas_call(
            functools.partial(kernel, ng, nx, ny, orb),
            out_shape=(
                pltpu.VMEM((e_count, 1, 2, orb, orb), BF),
                pltpu.VMEM((e_count, 1, 2, NB, NB), F32),
            ),
            in_specs=[any_space, any_space, any_space, any_space, smem, smem, vmem],
            out_specs=(vmem, vmem),
            scratch_shapes=[
                pltpu.VMEM((3, 2, 2, orb, orb), BF),
                pltpu.VMEM((2, 2, orb, orb), BF),
                pltpu.VMEM((orb, orb), BF),
                pltpu.VMEM((MODES, orb, orb), BF),
                pltpu.VMEM((4, orb, orb), F32),
                pltpu.VMEM((2, 2, orb, orb), BF),
                pltpu.VMEM((2, 2, orb, orb), BF),
                pltpu.VMEM((2, ny, NB, 2 * NB), BF),
                pltpu.VMEM((nx, NB, 2 * NB), F32),
                pltpu.VMEM((2 * NB, 2 * NB), BF),
                pltpu.VMEM((2, NB, 2 * NB), F32),
                pltpu.VMEM((2, NB, 2 * NB), F32),
                pltpu.VMEM((2, NB, 2 * NB), BF),
                dma((4,)),
                pltpu.SemaphoreType.REGULAR((4, rounds)),
                pltpu.SemaphoreType.REGULAR((1,)),
                dma((2, 3)),
                dma((2, 3)),
                dma((2, ny - 1)),
                dma((2, ny)),
                dma((nx - 1,)),
                dma((nx,)),
                dma((3,)),
                dma((2,)),
                dma((nx + ny - 2,)),
                dma((1,)),
            ],
            compiler_params=pltpu.CompilerParams(collective_id=0, has_side_effects=True),
        )(less, ret, ham, coup, occ, shf, face)

    in_specs = (
        P("energy", "slab", None, None, None),
        P("energy", "slab", None, None, None),
        P("slab", None, None),
        P(),
        P(),
        P(),
        P(),
    )
    out_specs = (P("energy", "slab", None, None, None), P("energy", "slab", None, None, None))
    return jax.shard_map(on_device, mesh=mesh, in_specs=in_specs, out_specs=out_specs, check_vma=False)
```
